32 devices in a mesh: chan: 8 (over y, x, core), win: 4 (over z).
Axes of the slice: x: 2, y: 2, z: 4, core: 2. Of those that a mesh axis runs over, the one named last changes fastest.
Arguments:
- records: float32 [16, 1024, 256], P('win', 'chan'), may hold values from -180 to 180
- sources: int32 [32], replicated, may hold values from 0 to 255, as said below
Outputs:
- correlations: float32 [32, 256, 256], P('win', None, 'chan')
The draws below stay inside these ranges and needn't reach their ends.
Inputs may be any that keep to these rules, and one draw needn't show every extreme that they name: `sources`: source s is one of the channels s * 8 to (s + 1) * 8 - 1; the first source is channel 0 and the last is channel 256 - 1.
All inputs are finite; a program needn't handle non-finite values.
Results may differ from the reference program's by a relative error of at most 0.00022.
Values sent between devices are 32-bit elements; how exact they have to be, the bound alone decides.
A program may use at most 64 MiB of HBM per device.

```python
import math
import jax
import jax.numpy as jnp
from jax import lax

L = 1024
W = 16
C = 256
NS = 32
LAGS = 256
HALF = 16
REACH = 32


def draw_records(key, part):
    subkeys = jax.random.split(key, 3)
    channel_gain = jnp.exp(jax.random.uniform(subkeys[0], (1, 1, C), minval=math.log(0.1), maxval=math.log(10.0)))
    segments = L // 16
    envelope = jnp.exp(jax.random.uniform(subkeys[1], (W, 16, C), minval=math.log(0.3), maxval=math.log(3.0)))
    envelope = jnp.repeat(envelope, segments, axis=1)
    random_part = jax.random.truncated_normal(subkeys[2], -6.0, 6.0, (W, L, C))
    return (channel_gain * envelope * random_part).astype(jnp.float32)


def draw_sources(key, part):
    spacing = C // NS
    offsets = jax.random.randint(key, (NS,), 0, spacing).astype(jnp.int32)
    offsets = offsets.at[0].set(0).at[NS - 1].set(spacing - 1)
    return (jnp.arange(NS, dtype=jnp.int32) * spacing + offsets).astype(jnp.int32)


def setup_inputs(seed: int = 0) -> dict:
    arg_keys = jax.random.split(jax.random.key(seed), 3)
    records = draw_records(jax.random.fold_in(arg_keys[2], 71), 0)
    sources = draw_sources(jax.random.fold_in(arg_keys[2], 71), 0)
    return {"records": records, "sources": sources}


HIGHEST = lax.Precision.HIGHEST
AMPLITUDE_FLOOR = 0.25
WHITE_EPSILON = 1e-06

def fourier_table(length):
    freq_count = length // 2
    freqs = jnp.arange(freq_count, dtype=jnp.int32)[:, None]
    sample_index = jnp.arange(length, dtype=jnp.int32)[None, :]
    angles = (freqs * sample_index % length).astype(jnp.float32) * (2.0 * math.pi / length)
    return jnp.concatenate([jnp.cos(angles), -jnp.sin(angles)], axis=0)

def band_table(freq_count, reach):
    rows_index = jnp.arange(freq_count, dtype=jnp.int32)[:, None]
    cols_index = jnp.arange(freq_count, dtype=jnp.int32)[None, :]
    return (jnp.abs(rows_index - cols_index) <= reach).astype(jnp.float32)

def inverse_table(length, lag_count, first_bin, bin_count, factor):
    freqs = first_bin + jnp.arange(bin_count, dtype=jnp.int32)
    lag_index = jnp.arange(lag_count, dtype=jnp.int32) - lag_count // 2
    angles = (lag_index[:, None] * freqs[None, :] % length).astype(jnp.float32) * (2.0 * math.pi / length)
    weights = jnp.where(freqs == 0, 1.0, 2.0).astype(jnp.float32)[None, :] * factor
    return jnp.concatenate([weights * jnp.cos(angles), -weights * jnp.sin(angles)], axis=1)

def reference(records, sources):
    freq_count = L // 2
    forward = fourier_table(L)
    band_matrix = band_table(freq_count, REACH)
    window_span = 2 * HALF + 1

    def one_window(window_data):
        chans = window_data.shape[1]
        padded = jnp.pad(jnp.abs(window_data), ((HALF, HALF), (0, 0)))
        running = jnp.concatenate([jnp.zeros((1, chans), jnp.float32), jnp.cumsum(padded, axis=0)], axis=0)
        amplitude = (running[window_span:] - running[:L]) / window_span
        normalized = window_data / jnp.maximum(amplitude, AMPLITUDE_FLOOR)
        spectrum = jnp.dot(forward, normalized, precision=HIGHEST)
        real_part = spectrum[:freq_count]
        imag_part = spectrum[freq_count:]
        magnitude = jnp.sqrt(real_part * real_part + imag_part * imag_part)
        smoothed = jnp.dot(band_matrix, magnitude, precision=HIGHEST) / (2 * REACH + 1) + WHITE_EPSILON
        return jnp.stack([real_part / smoothed, imag_part / smoothed])
    source_white = lax.map(one_window, records[:, :, sources])

    def accumulate(carry, pair):
        window_data, source_part = pair
        whitened = one_window(window_data)
        source_real = source_part[0][:, :, None]
        source_imag = source_part[1][:, :, None]
        white_real = whitened[0][:, None, :]
        white_imag = whitened[1][:, None, :]
        cross_real = carry[0] + source_real * white_real + source_imag * white_imag
        cross_imag = carry[1] + source_real * white_imag - source_imag * white_real
        return ((cross_real, cross_imag), None)
    chans = records.shape[2]
    zeros_init = jnp.zeros((freq_count, NS, chans), jnp.float32)
    (cross_real, cross_imag), _ = lax.scan(accumulate, (zeros_init, zeros_init), (records, source_white))
    factor = 1.0 / math.sqrt(W * freq_count)
    table = inverse_table(L, LAGS, 0, freq_count, factor).reshape(LAGS, 2, freq_count)
    stacked = jnp.stack([cross_real, cross_imag])
    return jnp.einsum('tak,aksc->stc', table, stacked, precision=HIGHEST)
```

```python
import functools
import math

import jax
import jax.numpy as jnp
import numpy as np
from jax import lax
from jax.experimental import pallas as pl
from jax.experimental.pallas import tpu as pltpu
from jax.sharding import PartitionSpec as P

HIGHEST = lax.Precision.HIGHEST
AMPLITUDE_FLOOR = 0.25
WHITE_EPSILON = 1e-06


def fourier_table(length):
    freq_count = length // 2
    freqs = jnp.arange(freq_count, dtype=jnp.int32)[:, None]
    sample_index = jnp.arange(length, dtype=jnp.int32)[None, :]
    angles = (freqs * sample_index % length).astype(jnp.float32) * (2.0 * math.pi / length)
    return jnp.concatenate([jnp.cos(angles), -jnp.sin(angles)], axis=0)


def band_table(freq_count, reach):
    rows_index = jnp.arange(freq_count, dtype=jnp.int32)[:, None]
    cols_index = jnp.arange(freq_count, dtype=jnp.int32)[None, :]
    return (jnp.abs(rows_index - cols_index) <= reach).astype(jnp.float32)


def inverse_table(length, lag_count, first_bin, bin_count, factor):
    freqs = first_bin + jnp.arange(bin_count, dtype=jnp.int32)
    lag_index = jnp.arange(lag_count, dtype=jnp.int32) - lag_count // 2
    angles = (lag_index[:, None] * freqs[None, :] % length).astype(jnp.float32) * (
        2.0 * math.pi / length
    )
    weights = jnp.where(freqs == 0, 1.0, 2.0).astype(jnp.float32)[None, :] * factor
    return jnp.concatenate([weights * jnp.cos(angles), -weights * jnp.sin(angles)], axis=1)


def running_level(padded, time_count, window_span):
    window_total = padded.shape[0]
    chans = padded.shape[2]
    running = jnp.concatenate(
        [jnp.zeros((window_total, 1, chans), jnp.float32), jnp.cumsum(jnp.abs(padded), axis=1)],
        axis=1,
    )
    return (running[:, window_span:] - running[:, :time_count]) / window_span


def local(records, sources):
    chan_count = lax.axis_size("chan")
    local_windows, local_time, all_channels = records.shape
    length = local_time * chan_count
    freq_count = length // 2
    chan_width = all_channels // chan_count
    half_width = min(16, local_time)
    smooth_reach = length // 32
    window_span = 2 * half_width + 1
    lag_count = length // 4
    forward = fourier_table(length)
    band_matrix = band_table(freq_count, smooth_reach)
    pieces = lax.all_to_all(records, "chan", split_axis=2, concat_axis=1, tiled=True)
    padded = jnp.pad(pieces, ((0, 0), (half_width, half_width), (0, 0)))
    amplitude = running_level(padded, length, window_span)
    whiten_pieces = pieces / jnp.maximum(amplitude, AMPLITUDE_FLOOR)
    spectrum = jnp.einsum("kt,wtc->wkc", forward, whiten_pieces, precision=HIGHEST)
    real_part = spectrum[:, :freq_count]
    imag_part = spectrum[:, freq_count:]
    magnitude = jnp.sqrt(real_part * real_part + imag_part * imag_part)
    smoothed = (
        jnp.einsum("jk,wkc->wjc", band_matrix, magnitude, precision=HIGHEST)
        / (2 * smooth_reach + 1)
        + WHITE_EPSILON
    )
    whitened = jnp.stack([real_part / smoothed, imag_part / smoothed], axis=1)
    band_data = lax.all_to_all(whitened, "win", split_axis=2, concat_axis=0, tiled=True)
    total_windows = band_data.shape[0]
    band_count = band_data.shape[2]
    source_count = sources.shape[0]
    chan_index = lax.axis_index("chan")
    channel_ids = jnp.arange(chan_width, dtype=jnp.int32)
    per_device = source_count // chan_count
    owned_local = (
        lax.dynamic_slice_in_dim(sources, chan_index * per_device, per_device)
        - chan_index * chan_width
    )
    selector = (owned_local[:, None] == channel_ids[None, :]).astype(jnp.float32)
    chosen = jnp.einsum("sc,wafc->wafs", selector, band_data, precision=HIGHEST)
    spectra = lax.all_gather(chosen, "chan", axis=3, tiled=True)
    source_real = spectra[:, 0]
    source_imag = spectra[:, 1]
    white_real = band_data[:, 0]
    white_imag = band_data[:, 1]
    cross_real = jnp.einsum(
        "wfs,wfc->fsc", source_real, white_real, precision=HIGHEST
    ) + jnp.einsum("wfs,wfc->fsc", source_imag, white_imag, precision=HIGHEST)
    cross_imag = jnp.einsum(
        "wfs,wfc->fsc", source_real, white_imag, precision=HIGHEST
    ) - jnp.einsum("wfs,wfc->fsc", source_imag, white_real, precision=HIGHEST)
    stacked = jnp.stack([cross_real, cross_imag])
    factor = 1.0 / math.sqrt(total_windows * freq_count)
    band_start = lax.axis_index("win") * band_count
    band_table_part = inverse_table(length, lag_count, band_start, band_count, factor).reshape(
        lag_count, 2, band_count
    )
    return lax.psum_scatter(
        jnp.einsum("tak,aksc->stc", band_table_part, stacked, precision=HIGHEST),
        "win",
        scatter_dimension=0,
        tiled=True,
    )


LANES = 128
BF16 = jnp.bfloat16
MESH = pl.DeviceIdType.MESH


def bin_order(freq_count):
    per = freq_count // 8
    pairs = ((0, 4), (1, 7), (2, 6), (3, 5))
    return np.concatenate([8 * np.arange(per) + m for pair in pairs for m in pair])


def split_table(table):
    high = table.astype(np.float32).astype(BF16)
    low = (table - high.astype(np.float64)).astype(np.float32).astype(BF16)
    return np.stack([high, low])


def forward_blocks(length, time):
    per = length // 16
    rows = np.arange(time)[:, None]
    blocks = []
    for first, second in ((0, 4), (1, 7), (2, 6), (3, 5)):
        angle1 = 2 * np.pi * ((8 * np.arange(per) + first)[None, :] * rows % length) / length
        angle2 = 2 * np.pi * ((8 * np.arange(per) + second)[None, :] * rows % length) / length
        c1, s1, c2, s2 = np.cos(angle1), np.sin(angle1), np.cos(angle2), np.sin(angle2)
        if first == 0:
            zero = np.zeros_like(c1)
            top = np.concatenate([c1, zero, -s1, zero], axis=1)
            low = np.concatenate([zero, c2, zero, -s2], axis=1)
        else:
            top = np.concatenate([c1, c2, -s1, -s2], axis=1)
            low = np.concatenate([s1, -s2, c1, -c2], axis=1)
        blocks.append(np.concatenate([top, low], axis=0))
    return split_table(np.stack(blocks))


def smooth_table(freq_count, reach):
    order = bin_order(freq_count)
    return (np.abs(order[:, None] - order[None, :]) <= reach).astype(np.float32).astype(BF16)


def lag_table(length, lag_count, factor):
    bins = bin_order(length // 2)[:, None]
    lags = (np.arange(lag_count) - lag_count // 2)[None, :]
    angle = 2 * np.pi * (bins * lags % length) / length
    weight = np.where(bins == 0, 1.0, 2.0) * factor
    return split_table(np.concatenate([weight * np.cos(angle), -weight * np.sin(angle)], axis=0))


def halves(value):
    high = value.astype(BF16)
    return high, (value - high.astype(jnp.float32)).astype(BF16)


def dot(a, b):
    return jnp.dot(a, b, preferred_element_type=jnp.float32)


def fused_kernel(
    half_width, smooth_reach, chan_count, win_count, per_device,
    src_ref, rec_ref, fwd_hbm, band_hbm, lag_hbm, out_ref,
    xt, recv, nrm, yh, yl, mh, ml, wr, wi, gs, ch, cl, part, from_left, from_right,
    fwd, band, lag,
    tab_sem, a_send, a_recv, g_send, g_recv, r_send, left_sem, right_sem,
):
    me = lax.axis_index("chan")
    row = lax.axis_index("win")
    windows, time, _ = rec_ref.shape
    rows = recv.shape[1]
    width = rows // windows
    freq = wr.shape[1]
    tiles = freq // LANES

    tables = [
        pltpu.make_async_copy(hbm, vmem, tab_sem.at[i])
        for i, (hbm, vmem) in enumerate(((fwd_hbm, fwd), (band_hbm, band), (lag_hbm, lag)))
    ]
    for copy in tables:
        copy.start()
    barrier = pltpu.get_barrier_semaphore()
    for d in range(1, chan_count):
        pl.semaphore_signal(
            barrier, inc=1, device_id={"chan": lax.rem(me + d, chan_count)}, device_id_type=MESH
        )
    for d in range(1, win_count):
        pl.semaphore_signal(
            barrier, inc=1, device_id={"win": lax.rem(row + d, win_count)}, device_id_type=MESH
        )
    for w in range(windows):
        for h in range(rec_ref.shape[2] // LANES):
            tile = rec_ref[w, :, h * LANES : (h + 1) * LANES].T
            for i in range(LANES // width):
                xt[h * (LANES // width) + i, w * width : (w + 1) * width, :] = tile[
                    i * width : (i + 1) * width
                ]
    pl.semaphore_wait(barrier, chan_count + win_count - 2)

    exchange = []
    for d in range(1, chan_count):
        peer = lax.rem(me + d, chan_count)
        copy = pltpu.make_async_remote_copy(
            src_ref=xt.at[peer], dst_ref=recv.at[me], send_sem=a_send.at[d], recv_sem=a_recv.at[d],
            device_id={"chan": peer}, device_id_type=MESH,
        )
        copy.start()
        exchange.append(copy)
    recv[me] = xt[me]
    near_row = lax.broadcasted_iota(jnp.int32, (3 * time, time), 0) - time
    near_col = lax.broadcasted_iota(jnp.int32, (3 * time, time), 1)
    near = (jnp.abs(near_row - near_col) <= half_width).astype(jnp.float32).astype(BF16)
    for copy in exchange:
        copy.wait_recv()

    for i in range(8):
        lo, hi = max(i - 1, 0), min(i + 1, 7)
        level = jnp.zeros((rows, time), jnp.float32)
        for j in range(lo, hi + 1):
            high, low = halves(jnp.abs(recv[j]))
            weights = near[(j - i + 1) * time : (j - i + 2) * time]
            level = level + (dot(high, weights) + dot(low, weights))
        level = level * (1.0 / (2 * half_width + 1))
        nrm[i] = recv[i] / jnp.maximum(level, AMPLITUDE_FLOOR)

    root = math.sqrt(0.5)

    def butterfly(block, _):
        at = pl.ds(pl.multiple_of(block * width, width), width)
        n = [nrm[i, at, :] for i in range(8)]
        a = [n[i] + n[i + 4] for i in range(4)]
        b = [n[i] - n[i + 4] for i in range(4)]
        even, odd = a[0] + a[2], a[1] + a[3]
        diff, total = root * (b[1] - b[3]), root * (b[1] + b[3])
        pairs = (
            (even + odd, even - odd),
            (b[0] + diff, -(b[2] + total)),
            (a[0] - a[2], a[3] - a[1]),
            (b[0] - diff, b[2] - total),
        )
        for g, pair in enumerate(pairs):
            for side, value in enumerate(pair):
                high, low = halves(value)
                yh[g, at, side * time : (side + 1) * time] = high
                yl[g, at, side * time : (side + 1) * time] = low
        return 0

    lax.fori_loop(0, windows, butterfly, 0)
    tables[0].wait()
    for g in range(4):
        at = slice(g * LANES, (g + 1) * LANES)
        both = dot(yh[g], fwd[0, g]) + dot(yl[g], fwd[0, g]) + dot(yh[g], fwd[1, g])
        real, imag = both[:, :LANES], both[:, LANES:]
        wr[:, at] = real
        wi[:, at] = imag
        high, low = halves(jnp.sqrt(real * real + imag * imag))
        mh[:, at] = high
        ml[:, at] = low
    tables[1].wait()
    for g in range(freq // 256):
        at = slice(g * 256, (g + 1) * 256)
        smoothed = (dot(mh[...], band[:, at]) + dot(ml[...], band[:, at])) / (
            2 * smooth_reach + 1
        ) + WHITE_EPSILON
        wr[:, at] = wr[:, at] / smoothed
        wi[:, at] = wi[:, at] / smoothed

    for i in range(per_device):
        owned = lax.rem(src_ref[me * per_device + i], width)
        for w in range(windows):
            at = 2 * (windows * i + w)
            gs[me, at : at + 1, :] = wr[pl.ds(w * width + owned, 1), :]
            gs[me, at + 1 : at + 2, :] = wi[pl.ds(w * width + owned, 1), :]
    gather = []
    for d in range(1, chan_count):
        copy = pltpu.make_async_remote_copy(
            src_ref=gs.at[me], dst_ref=gs.at[me], send_sem=g_send.at[d], recv_sem=g_recv.at[d],
            device_id={"chan": lax.rem(me + d, chan_count)}, device_id_type=MESH,
        )
        copy.start()
        gather.append(copy)
    for copy in gather:
        copy.wait_recv()
    tables[2].wait()

    per_owner = chan_count // win_count
    upper = row // 2
    inner = lax.rem(row + upper, 2)

    def owner_of(p):
        lower = 3 - p + inner * (p // 2) * (2 * lax.rem(p, 2) - 1)
        return lower + upper * (3 - 2 * lower)

    def compute(owner):
        for t in range(tiles):
            at = slice(t * LANES, (t + 1) * LANES)
            white = [
                (wr[w * width : (w + 1) * width, at], wi[w * width : (w + 1) * width, at])
                for w in range(windows)
            ]
            for u in range(per_owner):
                for i in range(per_device):
                    real = imag = None
                    for w in range(windows):
                        line = 2 * (windows * i + w)
                        sr = gs[owner * per_owner + u, line : line + 1, at]
                        si = gs[owner * per_owner + u, line + 1 : line + 2, at]
                        r = sr * white[w][0] + si * white[w][1]
                        m = sr * white[w][1] - si * white[w][0]
                        real = r if real is None else real + r
                        imag = m if imag is None else imag + m
                    first = (u * per_device + i) * width
                    for side, value in enumerate((real, imag)):
                        high, low = halves(value)
                        col = side * freq + t * LANES
                        ch[first : first + width, col : col + LANES] = high
                        cl[first : first + width, col : col + LANES] = low
        part[owner] = dot(ch[...], lag[0]) + dot(cl[...], lag[0]) + dot(ch[...], lag[1])

    def hop(owner, source, landing, sem, target):
        return pltpu.make_async_remote_copy(
            src_ref=source, dst_ref=landing.at[owner], send_sem=r_send.at[owner],
            recv_sem=sem.at[owner], device_id={"win": target}, device_id_type=MESH,
        )

    def finish(owner):
        @pl.when(owner > row)
        def _():
            right = hop(owner, part.at[owner], from_left, left_sem, row + 1)

            @pl.when(row > 0)
            def _():
                right.wait_recv()
                part[owner] = part[owner] + from_left[owner]

            right.start()

        @pl.when(owner < row)
        def _():
            left = hop(owner, part.at[owner], from_right, right_sem, row - 1)

            @pl.when(row < win_count - 1)
            def _():
                left.wait_recv()
                part[owner] = part[owner] + from_right[owner]

            left.start()

    def step(p, _):
        compute(owner_of(p))

        @pl.when(inner == 0)
        def _():
            finish(owner_of(p))

        @pl.when((inner == 1) & (p > 0))
        def _():
            finish(owner_of(p - 1))

        return 0

    lax.fori_loop(0, win_count, step, 0)
    out_ref[...] = part[row]

    @pl.when(row > 0)
    def _():
        hop(row, part.at[row], from_left, left_sem, row - 1).wait_recv()
        out_ref[...] += from_left[row]

    @pl.when(row < win_count - 1)
    def _():
        hop(row, part.at[row], from_right, right_sem, row + 1).wait_recv()
        out_ref[...] += from_right[row]

    for copy in exchange + gather:
        copy.wait_send()
    for owner in range(win_count):
        @pl.when(row != owner)
        def _():
            hop(owner, part.at[owner], from_left, left_sem, lax.rem(row + 1, win_count)).wait_send()


def fused(records, sources):
    chan_count, win_count = lax.axis_size("chan"), lax.axis_size("win")
    windows, time, channels = records.shape
    length = time * chan_count
    freq = length // 2
    width = channels // chan_count
    rows = windows * width
    source_count = sources.shape[0]
    lag_count = length // 4
    reach = length // 32
    half_width = min(16, time)
    owned = source_count // win_count
    factor = 1.0 / math.sqrt(windows * win_count * freq)
    fwd = forward_blocks(length, time)
    band = smooth_table(freq, reach)
    lag = lag_table(length, lag_count, factor)
    f32 = jnp.float32
    block = owned * width
    per_device = source_count // chan_count
    vmem = pl.BlockSpec(memory_space=pltpu.VMEM)
    hbm = pl.BlockSpec(memory_space=pltpu.HBM)
    out = pl.pallas_call(
        functools.partial(fused_kernel, half_width, reach, chan_count, win_count, per_device),
        out_shape=jax.ShapeDtypeStruct((block, lag_count), f32),
        in_specs=[pl.BlockSpec(memory_space=pltpu.SMEM), vmem, hbm, hbm, hbm],
        out_specs=vmem,
        scratch_shapes=[
            pltpu.VMEM((chan_count, rows, time), f32),
            pltpu.VMEM((chan_count, rows, time), f32),
            pltpu.VMEM((chan_count, rows, time), f32),
            pltpu.VMEM((4, rows, 2 * time), BF16),
            pltpu.VMEM((4, rows, 2 * time), BF16),
            pltpu.VMEM((rows, freq), BF16),
            pltpu.VMEM((rows, freq), BF16),
            pltpu.VMEM((rows, freq), f32),
            pltpu.VMEM((rows, freq), f32),
            pltpu.VMEM((chan_count, 2 * windows * per_device, freq), f32),
            pltpu.VMEM((block, 2 * freq), BF16),
            pltpu.VMEM((block, 2 * freq), BF16),
            pltpu.VMEM((win_count, block, lag_count), f32),
            pltpu.VMEM((win_count, block, lag_count), f32),
            pltpu.VMEM((win_count, block, lag_count), f32),
            pltpu.VMEM(fwd.shape, BF16),
            pltpu.VMEM(band.shape, BF16),
            pltpu.VMEM(lag.shape, BF16),
            pltpu.SemaphoreType.DMA((3,)),
            pltpu.SemaphoreType.DMA((chan_count,)),
            pltpu.SemaphoreType.DMA((chan_count,)),
            pltpu.SemaphoreType.DMA((chan_count,)),
            pltpu.SemaphoreType.DMA((chan_count,)),
            pltpu.SemaphoreType.DMA((win_count,)),
            pltpu.SemaphoreType.DMA((win_count,)),
            pltpu.SemaphoreType.DMA((win_count,)),
        ],
        compiler_params=pltpu.CompilerParams(
            collective_id=0, has_side_effects=True, vmem_limit_bytes=48 * 1024 * 1024
        ),
        name="interferometry",
    )(sources, records, jnp.asarray(fwd), jnp.asarray(band), jnp.asarray(lag))
    return out.reshape(owned, width, lag_count).transpose(0, 2, 1)


def fits(records, sources):
    chan_count, win_count = lax.axis_size("chan"), lax.axis_size("win")
    time, channels = records.shape[1:]
    width = channels // chan_count
    return (
        time == LANES and chan_count == 8 and win_count == 4 and channels % LANES == 0
        and LANES % width == 0 and width % 16 == 0 and sources.shape[0] % chan_count == 0
    )


def body(records, sources):
    return fused(records, sources) if fits(records, sources) else local(records, sources)


def solution(mesh):
    placed = (P("win", "chan", None), P())
    return jax.shard_map(
        body, mesh=mesh, in_specs=placed, out_specs=P("win", None, "chan"), check_vma=False
    )
```

```python
import functools
import math

import jax
import jax.numpy as jnp
import numpy as np
from jax import lax
from jax.experimental import pallas as pl
from jax.experimental.pallas import tpu as pltpu
from jax.sharding import PartitionSpec as P

HIGHEST = lax.Precision.HIGHEST
AMPLITUDE_FLOOR = 0.25
WHITE_EPSILON = 1e-06


def fourier_table(length):
    freq_count = length // 2
    freqs = jnp.arange(freq_count, dtype=jnp.int32)[:, None]
    sample_index = jnp.arange(length, dtype=jnp.int32)[None, :]
    angles = (freqs * sample_index % length).astype(jnp.float32) * (2.0 * math.pi / length)
    return jnp.concatenate([jnp.cos(angles), -jnp.sin(angles)], axis=0)


def band_table(freq_count, reach):
    rows_index = jnp.arange(freq_count, dtype=jnp.int32)[:, None]
    cols_index = jnp.arange(freq_count, dtype=jnp.int32)[None, :]
    return (jnp.abs(rows_index - cols_index) <= reach).astype(jnp.float32)


def inverse_table(length, lag_count, first_bin, bin_count, factor):
    freqs = first_bin + jnp.arange(bin_count, dtype=jnp.int32)
    lag_index = jnp.arange(lag_count, dtype=jnp.int32) - lag_count // 2
    angles = (lag_index[:, None] * freqs[None, :] % length).astype(jnp.float32) * (
        2.0 * math.pi / length
    )
    weights = jnp.where(freqs == 0, 1.0, 2.0).astype(jnp.float32)[None, :] * factor
    return jnp.concatenate([weights * jnp.cos(angles), -weights * jnp.sin(angles)], axis=1)


def running_level(padded, time_count, window_span):
    window_total = padded.shape[0]
    chans = padded.shape[2]
    running = jnp.concatenate(
        [jnp.zeros((window_total, 1, chans), jnp.float32), jnp.cumsum(jnp.abs(padded), axis=1)],
        axis=1,
    )
    return (running[:, window_span:] - running[:, :time_count]) / window_span


def local(records, sources):
    chan_count = lax.axis_size("chan")
    local_windows, local_time, all_channels = records.shape
    length = local_time * chan_count
    freq_count = length // 2
    chan_width = all_channels // chan_count
    half_width = min(16, local_time)
    smooth_reach = length // 32
    window_span = 2 * half_width + 1
    lag_count = length // 4
    forward = fourier_table(length)
    band_matrix = band_table(freq_count, smooth_reach)
    pieces = lax.all_to_all(records, "chan", split_axis=2, concat_axis=1, tiled=True)
    padded = jnp.pad(pieces, ((0, 0), (half_width, half_width), (0, 0)))
    amplitude = running_level(padded, length, window_span)
    whiten_pieces = pieces / jnp.maximum(amplitude, AMPLITUDE_FLOOR)
    spectrum = jnp.einsum("kt,wtc->wkc", forward, whiten_pieces, precision=HIGHEST)
    real_part = spectrum[:, :freq_count]
    imag_part = spectrum[:, freq_count:]
    magnitude = jnp.sqrt(real_part * real_part + imag_part * imag_part)
    smoothed = (
        jnp.einsum("jk,wkc->wjc", band_matrix, magnitude, precision=HIGHEST)
        / (2 * smooth_reach + 1)
        + WHITE_EPSILON
    )
    whitened = jnp.stack([real_part / smoothed, imag_part / smoothed], axis=1)
    band_data = lax.all_to_all(whitened, "win", split_axis=2, concat_axis=0, tiled=True)
    total_windows = band_data.shape[0]
    band_count = band_data.shape[2]
    source_count = sources.shape[0]
    chan_index = lax.axis_index("chan")
    channel_ids = jnp.arange(chan_width, dtype=jnp.int32)
    per_device = source_count // chan_count
    owned_local = (
        lax.dynamic_slice_in_dim(sources, chan_index * per_device, per_device)
        - chan_index * chan_width
    )
    selector = (owned_local[:, None] == channel_ids[None, :]).astype(jnp.float32)
    chosen = jnp.einsum("sc,wafc->wafs", selector, band_data, precision=HIGHEST)
    spectra = lax.all_gather(chosen, "chan", axis=3, tiled=True)
    source_real = spectra[:, 0]
    source_imag = spectra[:, 1]
    white_real = band_data[:, 0]
    white_imag = band_data[:, 1]
    cross_real = jnp.einsum(
        "wfs,wfc->fsc", source_real, white_real, precision=HIGHEST
    ) + jnp.einsum("wfs,wfc->fsc", source_imag, white_imag, precision=HIGHEST)
    cross_imag = jnp.einsum(
        "wfs,wfc->fsc", source_real, white_imag, precision=HIGHEST
    ) - jnp.einsum("wfs,wfc->fsc", source_imag, white_real, precision=HIGHEST)
    stacked = jnp.stack([cross_real, cross_imag])
    factor = 1.0 / math.sqrt(total_windows * freq_count)
    band_start = lax.axis_index("win") * band_count
    band_table_part = inverse_table(length, lag_count, band_start, band_count, factor).reshape(
        lag_count, 2, band_count
    )
    return lax.psum_scatter(
        jnp.einsum("tak,aksc->stc", band_table_part, stacked, precision=HIGHEST),
        "win",
        scatter_dimension=0,
        tiled=True,
    )


LANES = 128
BF16 = jnp.bfloat16
MESH = pl.DeviceIdType.MESH


def bin_order(freq_count):
    per = freq_count // 8
    pairs = ((0, 4), (1, 7), (2, 6), (3, 5))
    return np.concatenate([8 * np.arange(per) + m for pair in pairs for m in pair])


def split_table(table):
    high = table.astype(np.float32).astype(BF16)
    low = (table - high.astype(np.float64)).astype(np.float32).astype(BF16)
    return np.stack([high, low])


def forward_blocks(length, time):
    per = length // 16
    rows = np.arange(time)[:, None]
    blocks = []
    for first, second in ((0, 4), (1, 7), (2, 6), (3, 5)):
        angle1 = 2 * np.pi * ((8 * np.arange(per) + first)[None, :] * rows % length) / length
        angle2 = 2 * np.pi * ((8 * np.arange(per) + second)[None, :] * rows % length) / length
        c1, s1, c2, s2 = np.cos(angle1), np.sin(angle1), np.cos(angle2), np.sin(angle2)
        if first == 0:
            zero = np.zeros_like(c1)
            top = np.concatenate([c1, zero, -s1, zero], axis=1)
            low = np.concatenate([zero, c2, zero, -s2], axis=1)
        else:
            top = np.concatenate([c1, c2, -s1, -s2], axis=1)
            low = np.concatenate([s1, -s2, c1, -c2], axis=1)
        blocks.append(np.concatenate([top, low], axis=0))
    return split_table(np.stack(blocks))


def smooth_table(freq_count, reach):
    order = bin_order(freq_count)
    return (np.abs(order[:, None] - order[None, :]) <= reach).astype(np.float32).astype(BF16)


def lag_table(length, lag_count, factor):
    bins = bin_order(length // 2)[:, None]
    lags = (np.arange(lag_count) - lag_count // 2)[None, :]
    angle = 2 * np.pi * (bins * lags % length) / length
    weight = np.where(bins == 0, 1.0, 2.0) * factor
    return split_table(np.concatenate([weight * np.cos(angle), -weight * np.sin(angle)], axis=0))


def halves(value):
    high = value.astype(BF16)
    return high, (value - high.astype(jnp.float32)).astype(BF16)


def dot(a, b):
    return jnp.dot(a, b, preferred_element_type=jnp.float32)


def fused_kernel(
    half_width, smooth_reach, chan_count, win_count, per_device,
    src_ref, rec_hbm, fwd_hbm, band_hbm, lag_hbm, out_ref,
    rec, xt, recv, nrm, yh, yl, mh, ml, wr, wi, gs, ch, cl, part, from_left, from_right,
    fwd, band, lag,
    rec_sem, tab_sem, a_send, a_recv, g_send, g_recv, r_send, left_sem, right_sem,
):
    me = lax.axis_index("chan")
    row = lax.axis_index("win")
    windows, time, _ = rec.shape
    rows = recv.shape[1]
    width = rows // windows
    freq = wr.shape[1]
    tiles = freq // LANES
    core, x, y = lax.rem(me, 2), lax.rem(me // 2, 2), me // 4
    upper = row // 2
    inner = lax.rem(row + upper, 2)

    def flipped(d):
        bits = ((core, 1), (x, 2), (y, 4))
        return me + sum(b * (1 - 2 * bit) for bit, b in bits if d & b)

    barrier = pltpu.get_barrier_semaphore()
    for d in range(1, chan_count):
        pl.semaphore_signal(barrier, inc=1, device_id={"chan": flipped(d)}, device_id_type=MESH)

    @pl.when(row > 0)
    def _():
        pl.semaphore_signal(barrier, inc=1, device_id={"win": row - 1}, device_id_type=MESH)

    @pl.when(row < win_count - 1)
    def _():
        pl.semaphore_signal(barrier, inc=1, device_id={"win": row + 1}, device_id_type=MESH)

    loads = [
        pltpu.make_async_copy(rec_hbm.at[w], rec.at[w], rec_sem.at[w]) for w in range(windows)
    ]
    tables = [
        pltpu.make_async_copy(hbm, vmem, tab_sem.at[i])
        for i, (hbm, vmem) in enumerate(((fwd_hbm, fwd), (band_hbm, band), (lag_hbm, lag)))
    ]
    for copy in loads + tables:
        copy.start()
    for w in range(windows):
        loads[w].wait()
        for h in range(rec.shape[2] // LANES):
            tile = rec[w, :, h * LANES : (h + 1) * LANES].T
            for i in range(LANES // width):
                xt[h * (LANES // width) + i, w * width : (w + 1) * width, :] = tile[
                    i * width : (i + 1) * width
                ]

    @pl.when(inner == 0)
    def _():
        pl.semaphore_wait(barrier, chan_count)

    @pl.when(inner == 1)
    def _():
        pl.semaphore_wait(barrier, chan_count + 1)

    exchange = []
    for d in (6, 7, 4, 5, 2, 3, 1):
        peer = flipped(d)
        copy = pltpu.make_async_remote_copy(
            src_ref=xt.at[peer], dst_ref=recv.at[me], send_sem=a_send.at[d], recv_sem=a_recv.at[d],
            device_id={"chan": peer}, device_id_type=MESH,
        )
        copy.start()
        exchange.append(copy)
    recv[me] = xt[me]
    near_row = lax.broadcasted_iota(jnp.int32, (3 * time, time), 0) - time
    near_col = lax.broadcasted_iota(jnp.int32, (3 * time, time), 1)
    near = (jnp.abs(near_row - near_col) <= half_width).astype(jnp.float32).astype(BF16)
    for copy in exchange:
        copy.wait_recv()

    for i in range(8):
        lo, hi = max(i - 1, 0), min(i + 1, 7)
        level = jnp.zeros((rows, time), jnp.float32)
        for j in range(lo, hi + 1):
            high, low = halves(jnp.abs(recv[j]))
            weights = near[(j - i + 1) * time : (j - i + 2) * time]
            level = level + (dot(high, weights) + dot(low, weights))
        level = level * (1.0 / (2 * half_width + 1))
        nrm[i] = recv[i] / jnp.maximum(level, AMPLITUDE_FLOOR)

    root = math.sqrt(0.5)

    def butterfly(block, _):
        at = pl.ds(pl.multiple_of(block * width, width), width)
        n = [nrm[i, at, :] for i in range(8)]
        a = [n[i] + n[i + 4] for i in range(4)]
        b = [n[i] - n[i + 4] for i in range(4)]
        even, odd = a[0] + a[2], a[1] + a[3]
        diff, total = root * (b[1] - b[3]), root * (b[1] + b[3])
        pairs = (
            (even + odd, even - odd),
            (b[0] + diff, -(b[2] + total)),
            (a[0] - a[2], a[3] - a[1]),
            (b[0] - diff, b[2] - total),
        )
        for g, pair in enumerate(pairs):
            for side, value in enumerate(pair):
                high, low = halves(value)
                yh[g, at, side * time : (side + 1) * time] = high
                yl[g, at, side * time : (side + 1) * time] = low
        return 0

    lax.fori_loop(0, windows, butterfly, 0)
    tables[0].wait()
    for g in range(4):
        at = slice(g * LANES, (g + 1) * LANES)
        both = dot(yh[g], fwd[0, g]) + dot(yl[g], fwd[0, g]) + dot(yh[g], fwd[1, g])
        real, imag = both[:, :LANES], both[:, LANES:]
        wr[:, at] = real
        wi[:, at] = imag
        high, low = halves(jnp.sqrt(real * real + imag * imag))
        mh[:, at] = high
        ml[:, at] = low
    tables[1].wait()
    for g in range(freq // 256):
        at = slice(g * 256, (g + 1) * 256)
        smoothed = (dot(mh[...], band[:, at]) + dot(ml[...], band[:, at])) / (
            2 * smooth_reach + 1
        ) + WHITE_EPSILON
        wr[:, at] = wr[:, at] / smoothed
        wi[:, at] = wi[:, at] / smoothed

    for i in range(per_device):
        owned = lax.rem(src_ref[me * per_device + i], width)
        for w in range(windows):
            at = 2 * (windows * i + w)
            gs[me, at : at + 1, :] = wr[pl.ds(w * width + owned, 1), :]
            gs[me, at + 1 : at + 2, :] = wi[pl.ds(w * width + owned, 1), :]
    gather = {}
    for d in (4, 5, 1, 6, 7, 2, 3):
        gather[d] = pltpu.make_async_remote_copy(
            src_ref=gs.at[me], dst_ref=gs.at[me], send_sem=g_send.at[d], recv_sem=g_recv.at[d],
            device_id={"chan": flipped(d)}, device_id_type=MESH,
        )
        gather[d].start()
    tables[2].wait()

    away = (1 - upper) * (1 - y) + upper * y

    def chunk_of(q):
        p, k = q // 2, lax.rem(q, 2)
        dx, late = lax.rem(p, 2), p // 2
        dy = away + late * (1 - 2 * away)
        owner = 2 * (y + dy * (1 - 2 * y)) + x + dx * (1 - 2 * x)
        return owner, core + k * (1 - 2 * core), 4 * dy + 2 * dx + k

    def compute(owner, half):
        device = owner * 2 + half
        for t in range(tiles):
            at = slice(t * LANES, (t + 1) * LANES)
            white = [
                (wr[w * width : (w + 1) * width, at], wi[w * width : (w + 1) * width, at])
                for w in range(windows)
            ]
            for i in range(per_device):
                real = imag = None
                for w in range(windows):
                    line = 2 * (windows * i + w)
                    sr = gs[device, line : line + 1, at]
                    si = gs[device, line + 1 : line + 2, at]
                    r = sr * white[w][0] + si * white[w][1]
                    m = sr * white[w][1] - si * white[w][0]
                    real = r if real is None else real + r
                    imag = m if imag is None else imag + m
                for side, value in enumerate((real, imag)):
                    high, low = halves(value)
                    col = side * freq + t * LANES
                    ch[i * width : (i + 1) * width, col : col + LANES] = high
                    cl[i * width : (i + 1) * width, col : col + LANES] = low
        part[device] = dot(ch[...], lag[0]) + dot(cl[...], lag[0]) + dot(ch[...], lag[1])

    def hop(slot, landing, sem, target):
        return pltpu.make_async_remote_copy(
            src_ref=part.at[slot], dst_ref=landing.at[slot], send_sem=r_send.at[slot],
            recv_sem=sem.at[slot], device_id={"win": target}, device_id_type=MESH,
        )

    def finish(owner, half):
        slot = owner * 2 + half

        @pl.when(owner > row)
        def _():
            right = hop(slot, from_left, left_sem, row + 1)

            @pl.when(row > 0)
            def _():
                right.wait_recv()
                part[slot] = part[slot] + from_left[slot]

            right.start()

        @pl.when(owner < row)
        def _():
            left = hop(slot, from_right, right_sem, row - 1)

            @pl.when(row < win_count - 1)
            def _():
                left.wait_recv()
                part[slot] = part[slot] + from_right[slot]

            left.start()

    def step(q, _):
        owner, half, d = chunk_of(q)

        @pl.when(d > 0)
        def _():
            pltpu.make_async_remote_copy(
                src_ref=gs.at[me], dst_ref=gs.at[me], send_sem=g_send.at[d], recv_sem=g_recv.at[d],
                device_id={"chan": lax.rem(me + 1, chan_count)}, device_id_type=MESH,
            ).wait_recv()

        compute(owner, half)

        @pl.when(inner == 0)
        def _():
            finish(owner, half)

        @pl.when((inner == 1) & (q >= 4) & (q < 6))
        def _():
            first, side, _ = chunk_of(q - 4)
            finish(first, side)

        return 0

    chunks = 2 * win_count
    lax.fori_loop(0, chunks, step, 0)

    back = 3 * upper

    def finish_back(when):
        @pl.when((inner == 1) & (when == 0))
        def _():
            for k in range(2):
                finish(back, core + k * (1 - 2 * core))

    parity = x + upper * (1 - 2 * x)
    finish_back(parity)

    @pl.when(inner == 1)
    def _():
        for q in (2, 3):
            owner, half, _ = chunk_of(q)
            finish(owner, half)

    finish_back(1 - parity)

    block = part.shape[1]
    for k in range(2):
        half = core + k * (1 - 2 * core)
        slot = row * 2 + half
        at = pl.ds(pl.multiple_of(half * block, block), block)
        out_ref[at, :] = part[slot]

        @pl.when(row < win_count - 1)
        def _():
            hop(slot, from_right, right_sem, row + 1).wait_recv()
            out_ref[at, :] += from_right[slot]

        @pl.when(row > 0)
        def _():
            hop(slot, from_left, left_sem, row - 1).wait_recv()
            out_ref[at, :] += from_left[slot]

    for copy in exchange + list(gather.values()):
        copy.wait_send()
    for slot in range(chunks):
        @pl.when(row != slot // 2)
        def _():
            hop(slot, from_left, left_sem, lax.rem(row + 1, win_count)).wait_send()


def fused(records, sources):
    chan_count, win_count = lax.axis_size("chan"), lax.axis_size("win")
    windows, time, channels = records.shape
    length = time * chan_count
    freq = length // 2
    width = channels // chan_count
    rows = windows * width
    source_count = sources.shape[0]
    lag_count = length // 4
    reach = length // 32
    half_width = min(16, time)
    owned = source_count // win_count
    factor = 1.0 / math.sqrt(windows * win_count * freq)
    fwd = forward_blocks(length, time)
    band = smooth_table(freq, reach)
    lag = lag_table(length, lag_count, factor)
    f32 = jnp.float32
    block = owned * width
    half = block // 2
    per_device = source_count // chan_count
    vmem = pl.BlockSpec(memory_space=pltpu.VMEM)
    hbm = pl.BlockSpec(memory_space=pltpu.HBM)
    out = pl.pallas_call(
        functools.partial(fused_kernel, half_width, reach, chan_count, win_count, per_device),
        out_shape=jax.ShapeDtypeStruct((block, lag_count), f32),
        in_specs=[pl.BlockSpec(memory_space=pltpu.SMEM), hbm, hbm, hbm, hbm],
        out_specs=vmem,
        scratch_shapes=[
            pltpu.VMEM(records.shape, f32),
            pltpu.VMEM((chan_count, rows, time), f32),
            pltpu.VMEM((chan_count, rows, time), f32),
            pltpu.VMEM((chan_count, rows, time), f32),
            pltpu.VMEM((4, rows, 2 * time), BF16),
            pltpu.VMEM((4, rows, 2 * time), BF16),
            pltpu.VMEM((rows, freq), BF16),
            pltpu.VMEM((rows, freq), BF16),
            pltpu.VMEM((rows, freq), f32),
            pltpu.VMEM((rows, freq), f32),
            pltpu.VMEM((chan_count, 2 * windows * per_device, freq), f32),
            pltpu.VMEM((half, 2 * freq), BF16),
            pltpu.VMEM((half, 2 * freq), BF16),
            pltpu.VMEM((2 * win_count, half, lag_count), f32),
            pltpu.VMEM((2 * win_count, half, lag_count), f32),
            pltpu.VMEM((2 * win_count, half, lag_count), f32),
            pltpu.VMEM(fwd.shape, BF16),
            pltpu.VMEM(band.shape, BF16),
            pltpu.VMEM(lag.shape, BF16),
            pltpu.SemaphoreType.DMA((windows,)),
            pltpu.SemaphoreType.DMA((3,)),
            pltpu.SemaphoreType.DMA((chan_count,)),
            pltpu.SemaphoreType.DMA((chan_count,)),
            pltpu.SemaphoreType.DMA((chan_count,)),
            pltpu.SemaphoreType.DMA((chan_count,)),
            pltpu.SemaphoreType.DMA((2 * win_count,)),
            pltpu.SemaphoreType.DMA((2 * win_count,)),
            pltpu.SemaphoreType.DMA((2 * win_count,)),
        ],
        compiler_params=pltpu.CompilerParams(
            collective_id=0, has_side_effects=True, vmem_limit_bytes=67_043_328
        ),
        name="interferometry",
    )(sources, records, jnp.asarray(fwd), jnp.asarray(band), jnp.asarray(lag))
    return out.reshape(owned, width, lag_count).transpose(0, 2, 1)


def fits(records, sources):
    chan_count, win_count = lax.axis_size("chan"), lax.axis_size("win")
    time, channels = records.shape[1:]
    width = channels // chan_count
    return (
        time == LANES and chan_count == 8 and win_count == 4 and channels % LANES == 0
        and LANES % width == 0 and width % 16 == 0 and sources.shape[0] % chan_count == 0
    )


def body(records, sources):
    return fused(records, sources) if fits(records, sources) else local(records, sources)


def solution(mesh):
    placed = (P("win", "chan", None), P())
    return jax.shard_map(
        body, mesh=mesh, in_specs=placed, out_specs=P("win", None, "chan"), check_vma=False
    )
```

```python
import functools
import math

import jax
import jax.numpy as jnp
import numpy as np
from jax import lax
from jax.experimental import pallas as pl
from jax.experimental.pallas import tpu as pltpu
from jax.sharding import PartitionSpec as P

HIGHEST = lax.Precision.HIGHEST
AMPLITUDE_FLOOR = 0.25
WHITE_EPSILON = 1e-06


def fourier_table(length):
    freq_count = length // 2
    freqs = jnp.arange(freq_count, dtype=jnp.int32)[:, None]
    sample_index = jnp.arange(length, dtype=jnp.int32)[None, :]
    angles = (freqs * sample_index % length).astype(jnp.float32) * (2.0 * math.pi / length)
    return jnp.concatenate([jnp.cos(angles), -jnp.sin(angles)], axis=0)


def band_table(freq_count, reach):
    rows_index = jnp.arange(freq_count, dtype=jnp.int32)[:, None]
    cols_index = jnp.arange(freq_count, dtype=jnp.int32)[None, :]
    return (jnp.abs(rows_index - cols_index) <= reach).astype(jnp.float32)


def inverse_table(length, lag_count, first_bin, bin_count, factor):
    freqs = first_bin + jnp.arange(bin_count, dtype=jnp.int32)
    lag_index = jnp.arange(lag_count, dtype=jnp.int32) - lag_count // 2
    angles = (lag_index[:, None] * freqs[None, :] % length).astype(jnp.float32) * (
        2.0 * math.pi / length
    )
    weights = jnp.where(freqs == 0, 1.0, 2.0).astype(jnp.float32)[None, :] * factor
    return jnp.concatenate([weights * jnp.cos(angles), -weights * jnp.sin(angles)], axis=1)


def running_level(padded, time_count, window_span):
    window_total = padded.shape[0]
    chans = padded.shape[2]
    running = jnp.concatenate(
        [jnp.zeros((window_total, 1, chans), jnp.float32), jnp.cumsum(jnp.abs(padded), axis=1)],
        axis=1,
    )
    return (running[:, window_span:] - running[:, :time_count]) / window_span


def local(records, sources):
    chan_count = lax.axis_size("chan")
    local_windows, local_time, all_channels = records.shape
    length = local_time * chan_count
    freq_count = length // 2
    chan_width = all_channels // chan_count
    half_width = min(16, local_time)
    smooth_reach = length // 32
    window_span = 2 * half_width + 1
    lag_count = length // 4
    forward = fourier_table(length)
    band_matrix = band_table(freq_count, smooth_reach)
    pieces = lax.all_to_all(records, "chan", split_axis=2, concat_axis=1, tiled=True)
    padded = jnp.pad(pieces, ((0, 0), (half_width, half_width), (0, 0)))
    amplitude = running_level(padded, length, window_span)
    whiten_pieces = pieces / jnp.maximum(amplitude, AMPLITUDE_FLOOR)
    spectrum = jnp.einsum("kt,wtc->wkc", forward, whiten_pieces, precision=HIGHEST)
    real_part = spectrum[:, :freq_count]
    imag_part = spectrum[:, freq_count:]
    magnitude = jnp.sqrt(real_part * real_part + imag_part * imag_part)
    smoothed = (
        jnp.einsum("jk,wkc->wjc", band_matrix, magnitude, precision=HIGHEST)
        / (2 * smooth_reach + 1)
        + WHITE_EPSILON
    )
    whitened = jnp.stack([real_part / smoothed, imag_part / smoothed], axis=1)
    band_data = lax.all_to_all(whitened, "win", split_axis=2, concat_axis=0, tiled=True)
    total_windows = band_data.shape[0]
    band_count = band_data.shape[2]
    source_count = sources.shape[0]
    chan_index = lax.axis_index("chan")
    channel_ids = jnp.arange(chan_width, dtype=jnp.int32)
    per_device = source_count // chan_count
    owned_local = (
        lax.dynamic_slice_in_dim(sources, chan_index * per_device, per_device)
        - chan_index * chan_width
    )
    selector = (owned_local[:, None] == channel_ids[None, :]).astype(jnp.float32)
    chosen = jnp.einsum("sc,wafc->wafs", selector, band_data, precision=HIGHEST)
    spectra = lax.all_gather(chosen, "chan", axis=3, tiled=True)
    source_real = spectra[:, 0]
    source_imag = spectra[:, 1]
    white_real = band_data[:, 0]
    white_imag = band_data[:, 1]
    cross_real = jnp.einsum(
        "wfs,wfc->fsc", source_real, white_real, precision=HIGHEST
    ) + jnp.einsum("wfs,wfc->fsc", source_imag, white_imag, precision=HIGHEST)
    cross_imag = jnp.einsum(
        "wfs,wfc->fsc", source_real, white_imag, precision=HIGHEST
    ) - jnp.einsum("wfs,wfc->fsc", source_imag, white_real, precision=HIGHEST)
    stacked = jnp.stack([cross_real, cross_imag])
    factor = 1.0 / math.sqrt(total_windows * freq_count)
    band_start = lax.axis_index("win") * band_count
    band_table_part = inverse_table(length, lag_count, band_start, band_count, factor).reshape(
        lag_count, 2, band_count
    )
    return lax.psum_scatter(
        jnp.einsum("tak,aksc->stc", band_table_part, stacked, precision=HIGHEST),
        "win",
        scatter_dimension=0,
        tiled=True,
    )


LANES = 128
PIECES = 2
BF16 = jnp.bfloat16
MESH = pl.DeviceIdType.MESH


def bin_order(freq_count):
    per = freq_count // 8
    pairs = ((0, 4), (1, 7), (2, 6), (3, 5))
    return np.concatenate([8 * np.arange(per) + m for pair in pairs for m in pair])


def split_table(table):
    high = table.astype(np.float32).astype(BF16)
    low = (table - high.astype(np.float64)).astype(np.float32).astype(BF16)
    return np.stack([high, low])


def forward_blocks(length, time):
    per = length // 16
    rows = np.arange(time)[:, None]
    blocks = []
    for first, second in ((0, 4), (1, 7), (2, 6), (3, 5)):
        angle1 = 2 * np.pi * ((8 * np.arange(per) + first)[None, :] * rows % length) / length
        angle2 = 2 * np.pi * ((8 * np.arange(per) + second)[None, :] * rows % length) / length
        c1, s1, c2, s2 = np.cos(angle1), np.sin(angle1), np.cos(angle2), np.sin(angle2)
        if first == 0:
            zero = np.zeros_like(c1)
            top = np.concatenate([c1, zero, -s1, zero], axis=1)
            low = np.concatenate([zero, c2, zero, -s2], axis=1)
        else:
            top = np.concatenate([c1, c2, -s1, -s2], axis=1)
            low = np.concatenate([s1, -s2, c1, -c2], axis=1)
        blocks.append(np.concatenate([top, low], axis=0))
    return split_table(np.stack(blocks))


def smooth_table(freq_count, reach):
    order = bin_order(freq_count)
    return (np.abs(order[:, None] - order[None, :]) <= reach).astype(np.float32).astype(BF16)


def lag_table(length, lag_count, factor):
    bins = bin_order(length // 2)[:, None]
    lags = (np.arange(lag_count) - lag_count // 2)[None, :]
    angle = 2 * np.pi * (bins * lags % length) / length
    weight = np.where(bins == 0, 1.0, 2.0) * factor
    return split_table(np.concatenate([weight * np.cos(angle), -weight * np.sin(angle)], axis=0))


def halves(value):
    high = value.astype(BF16)
    return high, (value - high.astype(jnp.float32)).astype(BF16)


def dot(a, b):
    return jnp.dot(a, b, preferred_element_type=jnp.float32)


def fused_kernel(
    half_width, smooth_reach, chan_count, win_count, per_device,
    src_ref, rec_hbm, fwd_hbm, band_hbm, lag_hbm, out_ref,
    rec, xt, recv, nrm, yh, yl, mh, ml, wr, wi, gs, ch, cl, part, from_left, from_right,
    fwd, band, lag,
    rec_sem, tab_sem, a_send, a_recv, g_send, g_recv, r_send, left_sem, right_sem,
):
    me = lax.axis_index("chan")
    row = lax.axis_index("win")
    windows, time, _ = rec.shape
    rows = recv.shape[1]
    width = rows // windows
    freq = wr.shape[1]
    tiles = freq // LANES
    core, x, y = lax.rem(me, 2), lax.rem(me // 2, 2), me // 4
    upper = row // 2
    inner = lax.rem(row + upper, 2)

    def flipped(d):
        bits = ((core, 1), (x, 2), (y, 4))
        return me + sum(b * (1 - 2 * bit) for bit, b in bits if d & b)

    barrier = pltpu.get_barrier_semaphore()
    for d in range(1, chan_count):
        pl.semaphore_signal(barrier, inc=1, device_id={"chan": flipped(d)}, device_id_type=MESH)

    @pl.when(row > 0)
    def _():
        pl.semaphore_signal(barrier, inc=1, device_id={"win": row - 1}, device_id_type=MESH)

    @pl.when(row < win_count - 1)
    def _():
        pl.semaphore_signal(barrier, inc=1, device_id={"win": row + 1}, device_id_type=MESH)

    loads = [
        pltpu.make_async_copy(rec_hbm.at[w], rec.at[w], rec_sem.at[w]) for w in range(windows)
    ]
    tables = [
        pltpu.make_async_copy(hbm, vmem, tab_sem.at[i])
        for i, (hbm, vmem) in enumerate(((fwd_hbm, fwd), (band_hbm, band), (lag_hbm, lag)))
    ]
    for copy in loads + tables:
        copy.start()
    for w in range(windows):
        loads[w].wait()
        for h in range(rec.shape[2] // LANES):
            tile = rec[w, :, h * LANES : (h + 1) * LANES].T
            for i in range(LANES // width):
                xt[h * (LANES // width) + i, w * width : (w + 1) * width, :] = tile[
                    i * width : (i + 1) * width
                ]

    @pl.when(inner == 0)
    def _():
        pl.semaphore_wait(barrier, chan_count)

    @pl.when(inner == 1)
    def _():
        pl.semaphore_wait(barrier, chan_count + 1)

    exchange = []
    for d in (6, 7, 4, 5, 2, 3, 1):
        peer = flipped(d)
        copy = pltpu.make_async_remote_copy(
            src_ref=xt.at[peer], dst_ref=recv.at[me], send_sem=a_send.at[d], recv_sem=a_recv.at[d],
            device_id={"chan": peer}, device_id_type=MESH,
        )
        copy.start()
        exchange.append(copy)
    recv[me] = xt[me]
    near_row = lax.broadcasted_iota(jnp.int32, (3 * time, time), 0) - time
    near_col = lax.broadcasted_iota(jnp.int32, (3 * time, time), 1)
    near = (jnp.abs(near_row - near_col) <= half_width).astype(jnp.float32).astype(BF16)
    for copy in exchange:
        copy.wait_recv()

    for i in range(8):
        lo, hi = max(i - 1, 0), min(i + 1, 7)
        level = jnp.zeros((rows, time), jnp.float32)
        for j in range(lo, hi + 1):
            high, low = halves(jnp.abs(recv[j]))
            weights = near[(j - i + 1) * time : (j - i + 2) * time]
            level = level + (dot(high, weights) + dot(low, weights))
        level = level * (1.0 / (2 * half_width + 1))
        nrm[i] = recv[i] / jnp.maximum(level, AMPLITUDE_FLOOR)

    root = math.sqrt(0.5)

    def butterfly(block, _):
        at = pl.ds(pl.multiple_of(block * width, width), width)
        n = [nrm[i, at, :] for i in range(8)]
        a = [n[i] + n[i + 4] for i in range(4)]
        b = [n[i] - n[i + 4] for i in range(4)]
        even, odd = a[0] + a[2], a[1] + a[3]
        diff, total = root * (b[1] - b[3]), root * (b[1] + b[3])
        pairs = (
            (even + odd, even - odd),
            (b[0] + diff, -(b[2] + total)),
            (a[0] - a[2], a[3] - a[1]),
            (b[0] - diff, b[2] - total),
        )
        for g, pair in enumerate(pairs):
            for side, value in enumerate(pair):
                high, low = halves(value)
                yh[g, at, side * time : (side + 1) * time] = high
                yl[g, at, side * time : (side + 1) * time] = low
        return 0

    lax.fori_loop(0, windows, butterfly, 0)
    tables[0].wait()
    for g in range(4):
        at = slice(g * LANES, (g + 1) * LANES)
        both = dot(yh[g], fwd[0, g]) + dot(yl[g], fwd[0, g]) + dot(yh[g], fwd[1, g])
        real, imag = both[:, :LANES], both[:, LANES:]
        wr[:, at] = real
        wi[:, at] = imag
        high, low = halves(jnp.sqrt(real * real + imag * imag))
        mh[:, at] = high
        ml[:, at] = low
    tables[1].wait()
    for g in range(freq // 256):
        at = slice(g * 256, (g + 1) * 256)
        smoothed = (dot(mh[...], band[:, at]) + dot(ml[...], band[:, at])) / (
            2 * smooth_reach + 1
        ) + WHITE_EPSILON
        wr[:, at] = wr[:, at] / smoothed
        wi[:, at] = wi[:, at] / smoothed

    for i in range(per_device):
        owned = lax.rem(src_ref[me * per_device + i], width)
        for w in range(windows):
            at = 2 * (windows * i + w)
            gs[me, at : at + 1, :] = wr[pl.ds(w * width + owned, 1), :]
            gs[me, at + 1 : at + 2, :] = wi[pl.ds(w * width + owned, 1), :]
    def passing(block, target):
        slot = gs.at[flipped(block)]
        return pltpu.make_async_remote_copy(
            src_ref=slot, dst_ref=slot, send_sem=g_send.at[block ^ target],
            recv_sem=g_recv.at[block ^ target], device_id={"chan": flipped(target)},
            device_id_type=MESH,
        )

    gather = {b ^ t: passing(b, t) for b, t in ((0, 4), (0, 2), (0, 1), (4, 1), (4, 2), (2, 1), (6, 1))}
    for d in (4, 2, 1):
        gather[d].start()
    tables[2].wait()

    away = (1 - upper) * (1 - y) + upper * y

    def chunk_of(q):
        p, k = q // 2, lax.rem(q, 2)
        dx, late = lax.rem(p, 2), p // 2
        dy = away + late * (1 - 2 * away)
        owner = 2 * (y + dy * (1 - 2 * y)) + x + dx * (1 - 2 * x)
        return owner, core + k * (1 - 2 * core), 4 * dy + 2 * dx + k

    def compute(owner, half):
        device = owner * 2 + half
        for t in range(tiles):
            at = slice(t * LANES, (t + 1) * LANES)
            white = [
                (wr[w * width : (w + 1) * width, at], wi[w * width : (w + 1) * width, at])
                for w in range(windows)
            ]
            for i in range(per_device):
                real = imag = None
                for w in range(windows):
                    line = 2 * (windows * i + w)
                    sr = gs[device, line : line + 1, at]
                    si = gs[device, line + 1 : line + 2, at]
                    r = sr * white[w][0] + si * white[w][1]
                    m = sr * white[w][1] - si * white[w][0]
                    real = r if real is None else real + r
                    imag = m if imag is None else imag + m
                for side, value in enumerate((real, imag)):
                    high, low = halves(value)
                    col = side * freq + t * LANES
                    ch[i * width : (i + 1) * width, col : col + LANES] = high
                    cl[i * width : (i + 1) * width, col : col + LANES] = low
        part[device] = dot(ch[...], lag[0]) + dot(cl[...], lag[0]) + dot(ch[...], lag[1])

    piece = part.shape[1] // PIECES

    def hop(slot, k, landing, sem, target):
        at = pl.ds(k * piece, piece)
        return pltpu.make_async_remote_copy(
            src_ref=part.at[slot, at], dst_ref=landing.at[slot, at],
            send_sem=r_send.at[slot * PIECES + k], recv_sem=sem.at[slot * PIECES + k],
            device_id={"win": target}, device_id_type=MESH,
        )

    def finish(owner, half):
        slot = owner * 2 + half

        @pl.when(owner > row)
        def _():
            for k in range(PIECES):
                right = hop(slot, k, from_left, left_sem, row + 1)

                @pl.when(row > 0)
                def _():
                    right.wait_recv()
                    at = slice(k * piece, (k + 1) * piece)
                    part[slot, at] = part[slot, at] + from_left[slot, at]

                right.start()

        @pl.when(owner < row)
        def _():
            for k in range(PIECES):
                left = hop(slot, k, from_right, right_sem, row - 1)

                @pl.when(row < win_count - 1)
                def _():
                    left.wait_recv()
                    at = slice(k * piece, (k + 1) * piece)
                    part[slot, at] = part[slot, at] + from_right[slot, at]

                left.start()

    def step(q, _):
        owner, half, d = chunk_of(q)

        @pl.when(q == 2 * (1 - away))
        def _():
            gather[4].wait_recv()
            gather[6].start()
            gather[5].start()
            gather[2].wait_recv()
            gather[3].start()

        @pl.when(q == 2 * (2 - away))
        def _():
            gather[6].wait_recv()
            gather[7].start()

        @pl.when(lax.rem(q, 2) == 1)
        def _():
            pltpu.make_async_remote_copy(
                src_ref=gs.at[me], dst_ref=gs.at[me], send_sem=g_send.at[d], recv_sem=g_recv.at[d],
                device_id={"chan": lax.rem(me + 1, chan_count)}, device_id_type=MESH,
            ).wait_recv()

        compute(owner, half)

        @pl.when(inner == 0)
        def _():
            finish(owner, half)

        @pl.when((inner == 1) & (q >= 2) & (q < 4))
        def _():
            first, side, _ = chunk_of(q - 2)
            finish(first, side)

        return 0

    chunks = 2 * win_count
    lax.fori_loop(0, chunks, step, 0)

    back = 3 * upper

    def finish_back(when):
        @pl.when((inner == 1) & (when == 0))
        def _():
            for k in range(2):
                finish(back, core + k * (1 - 2 * core))

    parity = x + upper * (1 - 2 * x)
    finish_back(parity)

    @pl.when(inner == 1)
    def _():
        for q in (2, 3):
            owner, half, _ = chunk_of(q)
            finish(owner, half)

    finish_back(1 - parity)

    block = part.shape[1]
    for k in range(2):
        half = core + k * (1 - 2 * core)
        slot = row * 2 + half
        at = pl.ds(pl.multiple_of(half * block, block), block)
        out_ref[at, :] = part[slot]

        @pl.when(row < win_count - 1)
        def _():
            for j in range(PIECES):
                hop(slot, j, from_right, right_sem, row + 1).wait_recv()
            out_ref[at, :] += from_right[slot]

        @pl.when(row > 0)
        def _():
            for j in range(PIECES):
                hop(slot, j, from_left, left_sem, row - 1).wait_recv()
            out_ref[at, :] += from_left[slot]

    for copy in exchange + list(gather.values()):
        copy.wait_send()
    for slot in range(chunks):
        @pl.when(row != slot // 2)
        def _():
            for k in range(PIECES):
                hop(slot, k, from_left, left_sem, lax.rem(row + 1, win_count)).wait_send()


def fused(records, sources):
    chan_count, win_count = lax.axis_size("chan"), lax.axis_size("win")
    windows, time, channels = records.shape
    length = time * chan_count
    freq = length // 2
    width = channels // chan_count
    rows = windows * width
    source_count = sources.shape[0]
    lag_count = length // 4
    reach = length // 32
    half_width = min(16, time)
    owned = source_count // win_count
    factor = 1.0 / math.sqrt(windows * win_count * freq)
    fwd = forward_blocks(length, time)
    band = smooth_table(freq, reach)
    lag = lag_table(length, lag_count, factor)
    f32 = jnp.float32
    block = owned * width
    half = block // 2
    per_device = source_count // chan_count
    vmem = pl.BlockSpec(memory_space=pltpu.VMEM)
    hbm = pl.BlockSpec(memory_space=pltpu.HBM)
    out = pl.pallas_call(
        functools.partial(fused_kernel, half_width, reach, chan_count, win_count, per_device),
        out_shape=jax.ShapeDtypeStruct((block, lag_count), f32),
        in_specs=[pl.BlockSpec(memory_space=pltpu.SMEM), hbm, hbm, hbm, hbm],
        out_specs=vmem,
        scratch_shapes=[
            pltpu.VMEM(records.shape, f32),
            pltpu.VMEM((chan_count, rows, time), f32),
            pltpu.VMEM((chan_count, rows, time), f32),
            pltpu.VMEM((chan_count, rows, time), f32),
            pltpu.VMEM((4, rows, 2 * time), BF16),
            pltpu.VMEM((4, rows, 2 * time), BF16),
            pltpu.VMEM((rows, freq), BF16),
            pltpu.VMEM((rows, freq), BF16),
            pltpu.VMEM((rows, freq), f32),
            pltpu.VMEM((rows, freq), f32),
            pltpu.VMEM((chan_count, 2 * windows * per_device, freq), f32),
            pltpu.VMEM((half, 2 * freq), BF16),
            pltpu.VMEM((half, 2 * freq), BF16),
            pltpu.VMEM((2 * win_count, half, lag_count), f32),
            pltpu.VMEM((2 * win_count, half, lag_count), f32),
            pltpu.VMEM((2 * win_count, half, lag_count), f32),
            pltpu.VMEM(fwd.shape, BF16),
            pltpu.VMEM(band.shape, BF16),
            pltpu.VMEM(lag.shape, BF16),
            pltpu.SemaphoreType.DMA((windows,)),
            pltpu.SemaphoreType.DMA((3,)),
            pltpu.SemaphoreType.DMA((chan_count,)),
            pltpu.SemaphoreType.DMA((chan_count,)),
            pltpu.SemaphoreType.DMA((chan_count,)),
            pltpu.SemaphoreType.DMA((chan_count,)),
            pltpu.SemaphoreType.DMA((2 * win_count * PIECES,)),
            pltpu.SemaphoreType.DMA((2 * win_count * PIECES,)),
            pltpu.SemaphoreType.DMA((2 * win_count * PIECES,)),
        ],
        compiler_params=pltpu.CompilerParams(
            collective_id=0, has_side_effects=True, vmem_limit_bytes=67_043_328
        ),
        name="interferometry",
    )(sources, records, jnp.asarray(fwd), jnp.asarray(band), jnp.asarray(lag))
    return out.reshape(owned, width, lag_count).transpose(0, 2, 1)


def fits(records, sources):
    chan_count, win_count = lax.axis_size("chan"), lax.axis_size("win")
    time, channels = records.shape[1:]
    width = channels // chan_count
    return (
        time == LANES and chan_count == 8 and win_count == 4 and channels % LANES == 0
        and LANES % width == 0 and width % 16 == 0 and sources.shape[0] % chan_count == 0
    )


def body(records, sources):
    return fused(records, sources) if fits(records, sources) else local(records, sources)


def solution(mesh):
    placed = (P("win", "chan", None), P())
    return jax.shard_map(
        body, mesh=mesh, in_specs=placed, out_specs=P("win", None, "chan"), check_vma=False
    )
```

```python
import functools
import math

import jax
import jax.numpy as jnp
import numpy as np
from jax import lax
from jax.experimental import pallas as pl
from jax.experimental.pallas import tpu as pltpu
from jax.sharding import PartitionSpec as P

HIGHEST = lax.Precision.HIGHEST
AMPLITUDE_FLOOR = 0.25
WHITE_EPSILON = 1e-06


def fourier_table(length):
    freq_count = length // 2
    freqs = jnp.arange(freq_count, dtype=jnp.int32)[:, None]
    sample_index = jnp.arange(length, dtype=jnp.int32)[None, :]
    angles = (freqs * sample_index % length).astype(jnp.float32) * (2.0 * math.pi / length)
    return jnp.concatenate([jnp.cos(angles), -jnp.sin(angles)], axis=0)


def band_table(freq_count, reach):
    rows_index = jnp.arange(freq_count, dtype=jnp.int32)[:, None]
    cols_index = jnp.arange(freq_count, dtype=jnp.int32)[None, :]
    return (jnp.abs(rows_index - cols_index) <= reach).astype(jnp.float32)


def inverse_table(length, lag_count, first_bin, bin_count, factor):
    freqs = first_bin + jnp.arange(bin_count, dtype=jnp.int32)
    lag_index = jnp.arange(lag_count, dtype=jnp.int32) - lag_count // 2
    angles = (lag_index[:, None] * freqs[None, :] % length).astype(jnp.float32) * (
        2.0 * math.pi / length
    )
    weights = jnp.where(freqs == 0, 1.0, 2.0).astype(jnp.float32)[None, :] * factor
    return jnp.concatenate([weights * jnp.cos(angles), -weights * jnp.sin(angles)], axis=1)


def running_level(padded, time_count, window_span):
    window_total = padded.shape[0]
    chans = padded.shape[2]
    running = jnp.concatenate(
        [jnp.zeros((window_total, 1, chans), jnp.float32), jnp.cumsum(jnp.abs(padded), axis=1)],
        axis=1,
    )
    return (running[:, window_span:] - running[:, :time_count]) / window_span


def local(records, sources):
    chan_count = lax.axis_size("chan")
    local_windows, local_time, all_channels = records.shape
    length = local_time * chan_count
    freq_count = length // 2
    chan_width = all_channels // chan_count
    half_width = min(16, local_time)
    smooth_reach = length // 32
    window_span = 2 * half_width + 1
    lag_count = length // 4
    forward = fourier_table(length)
    band_matrix = band_table(freq_count, smooth_reach)
    pieces = lax.all_to_all(records, "chan", split_axis=2, concat_axis=1, tiled=True)
    padded = jnp.pad(pieces, ((0, 0), (half_width, half_width), (0, 0)))
    amplitude = running_level(padded, length, window_span)
    whiten_pieces = pieces / jnp.maximum(amplitude, AMPLITUDE_FLOOR)
    spectrum = jnp.einsum("kt,wtc->wkc", forward, whiten_pieces, precision=HIGHEST)
    real_part = spectrum[:, :freq_count]
    imag_part = spectrum[:, freq_count:]
    magnitude = jnp.sqrt(real_part * real_part + imag_part * imag_part)
    smoothed = (
        jnp.einsum("jk,wkc->wjc", band_matrix, magnitude, precision=HIGHEST)
        / (2 * smooth_reach + 1)
        + WHITE_EPSILON
    )
    whitened = jnp.stack([real_part / smoothed, imag_part / smoothed], axis=1)
    band_data = lax.all_to_all(whitened, "win", split_axis=2, concat_axis=0, tiled=True)
    total_windows = band_data.shape[0]
    band_count = band_data.shape[2]
    source_count = sources.shape[0]
    chan_index = lax.axis_index("chan")
    channel_ids = jnp.arange(chan_width, dtype=jnp.int32)
    per_device = source_count // chan_count
    owned_local = (
        lax.dynamic_slice_in_dim(sources, chan_index * per_device, per_device)
        - chan_index * chan_width
    )
    selector = (owned_local[:, None] == channel_ids[None, :]).astype(jnp.float32)
    chosen = jnp.einsum("sc,wafc->wafs", selector, band_data, precision=HIGHEST)
    spectra = lax.all_gather(chosen, "chan", axis=3, tiled=True)
    source_real = spectra[:, 0]
    source_imag = spectra[:, 1]
    white_real = band_data[:, 0]
    white_imag = band_data[:, 1]
    cross_real = jnp.einsum(
        "wfs,wfc->fsc", source_real, white_real, precision=HIGHEST
    ) + jnp.einsum("wfs,wfc->fsc", source_imag, white_imag, precision=HIGHEST)
    cross_imag = jnp.einsum(
        "wfs,wfc->fsc", source_real, white_imag, precision=HIGHEST
    ) - jnp.einsum("wfs,wfc->fsc", source_imag, white_real, precision=HIGHEST)
    stacked = jnp.stack([cross_real, cross_imag])
    factor = 1.0 / math.sqrt(total_windows * freq_count)
    band_start = lax.axis_index("win") * band_count
    band_table_part = inverse_table(length, lag_count, band_start, band_count, factor).reshape(
        lag_count, 2, band_count
    )
    return lax.psum_scatter(
        jnp.einsum("tak,aksc->stc", band_table_part, stacked, precision=HIGHEST),
        "win",
        scatter_dimension=0,
        tiled=True,
    )


LANES = 128
PIECES = 4
BF16 = jnp.bfloat16
MESH = pl.DeviceIdType.MESH


def bin_order(freq_count):
    per = freq_count // 8
    pairs = ((0, 4), (1, 7), (2, 6), (3, 5))
    return np.concatenate([8 * np.arange(per) + m for pair in pairs for m in pair])


def split_table(table):
    high = table.astype(np.float32).astype(BF16)
    low = (table - high.astype(np.float64)).astype(np.float32).astype(BF16)
    return np.stack([high, low])


def forward_blocks(length, time):
    per = length // 16
    rows = np.arange(time)[:, None]
    blocks = []
    for first, second in ((0, 4), (1, 7), (2, 6), (3, 5)):
        angle1 = 2 * np.pi * ((8 * np.arange(per) + first)[None, :] * rows % length) / length
        angle2 = 2 * np.pi * ((8 * np.arange(per) + second)[None, :] * rows % length) / length
        c1, s1, c2, s2 = np.cos(angle1), np.sin(angle1), np.cos(angle2), np.sin(angle2)
        if first == 0:
            zero = np.zeros_like(c1)
            top = np.concatenate([c1, zero, -s1, zero], axis=1)
            low = np.concatenate([zero, c2, zero, -s2], axis=1)
        else:
            top = np.concatenate([c1, c2, -s1, -s2], axis=1)
            low = np.concatenate([s1, -s2, c1, -c2], axis=1)
        blocks.append(np.concatenate([top, low], axis=0))
    return split_table(np.stack(blocks))


def smooth_table(freq_count, reach):
    order = bin_order(freq_count)
    return (np.abs(order[:, None] - order[None, :]) <= reach).astype(np.float32).astype(BF16)


def lag_table(length, lag_count, factor):
    bins = bin_order(length // 2)[:, None]
    lags = (np.arange(lag_count) - lag_count // 2)[None, :]
    angle = 2 * np.pi * (bins * lags % length) / length
    weight = np.where(bins == 0, 1.0, 2.0) * factor
    return split_table(np.concatenate([weight * np.cos(angle), -weight * np.sin(angle)], axis=0))


def halves(value):
    high = value.astype(BF16)
    return high, (value - high.astype(jnp.float32)).astype(BF16)


def dot(a, b):
    return jnp.dot(a, b, preferred_element_type=jnp.float32)


def fused_kernel(
    half_width, smooth_reach, chan_count, win_count, per_device,
    src_ref, rec_hbm, fwd_hbm, band_hbm, lag_hbm, out_ref,
    rec, xt, recv, nrm, yh, yl, mh, ml, wr, wi, gs, ch, cl, part, from_left, from_right,
    fwd, band, lag,
    rec_sem, tab_sem, a_send, a_recv, g_send, g_recv, r_send, left_sem, right_sem,
):
    me = lax.axis_index("chan")
    row = lax.axis_index("win")
    windows, time, _ = rec.shape
    rows = recv.shape[1]
    width = rows // windows
    freq = wr.shape[1]
    tiles = freq // LANES
    core, x, y = lax.rem(me, 2), lax.rem(me // 2, 2), me // 4
    upper = row // 2
    inner = lax.rem(row + upper, 2)

    def flipped(d):
        bits = ((core, 1), (x, 2), (y, 4))
        return me + sum(b * (1 - 2 * bit) for bit, b in bits if d & b)

    barrier = pltpu.get_barrier_semaphore()
    for d in range(1, chan_count):
        pl.semaphore_signal(barrier, inc=1, device_id={"chan": flipped(d)}, device_id_type=MESH)

    @pl.when(row > 0)
    def _():
        pl.semaphore_signal(barrier, inc=1, device_id={"win": row - 1}, device_id_type=MESH)

    @pl.when(row < win_count - 1)
    def _():
        pl.semaphore_signal(barrier, inc=1, device_id={"win": row + 1}, device_id_type=MESH)

    loads = [
        pltpu.make_async_copy(rec_hbm.at[w], rec.at[w], rec_sem.at[w]) for w in range(windows)
    ]
    tables = [
        pltpu.make_async_copy(hbm, vmem, tab_sem.at[i])
        for i, (hbm, vmem) in enumerate(((fwd_hbm, fwd), (band_hbm, band), (lag_hbm, lag)))
    ]
    for copy in loads + tables:
        copy.start()
    for w in range(windows):
        loads[w].wait()
        for h in range(rec.shape[2] // LANES):
            tile = rec[w, :, h * LANES : (h + 1) * LANES].T
            for i in range(LANES // width):
                xt[h * (LANES // width) + i, w * width : (w + 1) * width, :] = tile[
                    i * width : (i + 1) * width
                ]

    @pl.when(inner == 0)
    def _():
        pl.semaphore_wait(barrier, chan_count)

    @pl.when(inner == 1)
    def _():
        pl.semaphore_wait(barrier, chan_count + 1)

    exchange = []
    for d in (6, 7, 4, 5, 2, 3, 1):
        peer = flipped(d)
        copy = pltpu.make_async_remote_copy(
            src_ref=xt.at[peer], dst_ref=recv.at[me], send_sem=a_send.at[d], recv_sem=a_recv.at[d],
            device_id={"chan": peer}, device_id_type=MESH,
        )
        copy.start()
        exchange.append(copy)
    recv[me] = xt[me]
    near_row = lax.broadcasted_iota(jnp.int32, (3 * time, time), 0) - time
    near_col = lax.broadcasted_iota(jnp.int32, (3 * time, time), 1)
    near = (jnp.abs(near_row - near_col) <= half_width).astype(jnp.float32).astype(BF16)
    for copy in exchange:
        copy.wait_recv()

    for i in range(8):
        lo, hi = max(i - 1, 0), min(i + 1, 7)
        level = jnp.zeros((rows, time), jnp.float32)
        for j in range(lo, hi + 1):
            high, low = halves(jnp.abs(recv[j]))
            weights = near[(j - i + 1) * time : (j - i + 2) * time]
            level = level + (dot(high, weights) + dot(low, weights))
        level = level * (1.0 / (2 * half_width + 1))
        nrm[i] = recv[i] / jnp.maximum(level, AMPLITUDE_FLOOR)

    root = math.sqrt(0.5)

    def butterfly(block, _):
        at = pl.ds(pl.multiple_of(block * width, width), width)
        n = [nrm[i, at, :] for i in range(8)]
        a = [n[i] + n[i + 4] for i in range(4)]
        b = [n[i] - n[i + 4] for i in range(4)]
        even, odd = a[0] + a[2], a[1] + a[3]
        diff, total = root * (b[1] - b[3]), root * (b[1] + b[3])
        pairs = (
            (even + odd, even - odd),
            (b[0] + diff, -(b[2] + total)),
            (a[0] - a[2], a[3] - a[1]),
            (b[0] - diff, b[2] - total),
        )
        for g, pair in enumerate(pairs):
            for side, value in enumerate(pair):
                high, low = halves(value)
                yh[g, at, side * time : (side + 1) * time] = high
                yl[g, at, side * time : (side + 1) * time] = low
        return 0

    lax.fori_loop(0, windows, butterfly, 0)
    tables[0].wait()
    for g in range(4):
        at = slice(g * LANES, (g + 1) * LANES)
        both = dot(yh[g], fwd[0, g]) + dot(yl[g], fwd[0, g]) + dot(yh[g], fwd[1, g])
        real, imag = both[:, :LANES], both[:, LANES:]
        wr[:, at] = real
        wi[:, at] = imag
        high, low = halves(jnp.sqrt(real * real + imag * imag))
        mh[:, at] = high
        ml[:, at] = low
    tables[1].wait()
    for g in range(freq // 256):
        at = slice(g * 256, (g + 1) * 256)
        smoothed = (dot(mh[...], band[:, at]) + dot(ml[...], band[:, at])) / (
            2 * smooth_reach + 1
        ) + WHITE_EPSILON
        wr[:, at] = wr[:, at] / smoothed
        wi[:, at] = wi[:, at] / smoothed

    for i in range(per_device):
        owned = lax.rem(src_ref[me * per_device + i], width)
        for w in range(windows):
            at = 2 * (windows * i + w)
            gs[me, at : at + 1, :] = wr[pl.ds(w * width + owned, 1), :]
            gs[me, at + 1 : at + 2, :] = wi[pl.ds(w * width + owned, 1), :]
    def passing(block, target):
        slot = gs.at[flipped(block)]
        return pltpu.make_async_remote_copy(
            src_ref=slot, dst_ref=slot, send_sem=g_send.at[block ^ target],
            recv_sem=g_recv.at[block ^ target], device_id={"chan": flipped(target)},
            device_id_type=MESH,
        )

    gather = {b ^ t: passing(b, t) for b, t in ((0, 4), (0, 2), (0, 1), (4, 1), (4, 2), (2, 1), (6, 1))}
    for d in (4, 2, 1):
        gather[d].start()
    tables[2].wait()

    away = (1 - upper) * (1 - y) + upper * y

    def chunk_of(q):
        p, k = q // 2, lax.rem(q, 2)
        dx, late = lax.rem(p, 2), p // 2
        dy = away + late * (1 - 2 * away)
        owner = 2 * (y + dy * (1 - 2 * y)) + x + dx * (1 - 2 * x)
        return owner, core + k * (1 - 2 * core), 4 * dy + 2 * dx + k

    def compute(owner, half):
        device = owner * 2 + half
        for t in range(tiles):
            at = slice(t * LANES, (t + 1) * LANES)
            white = [
                (wr[w * width : (w + 1) * width, at], wi[w * width : (w + 1) * width, at])
                for w in range(windows)
            ]
            for i in range(per_device):
                real = imag = None
                for w in range(windows):
                    line = 2 * (windows * i + w)
                    sr = gs[device, line : line + 1, at]
                    si = gs[device, line + 1 : line + 2, at]
                    r = sr * white[w][0] + si * white[w][1]
                    m = sr * white[w][1] - si * white[w][0]
                    real = r if real is None else real + r
                    imag = m if imag is None else imag + m
                for side, value in enumerate((real, imag)):
                    high, low = halves(value)
                    col = side * freq + t * LANES
                    ch[i * width : (i + 1) * width, col : col + LANES] = high
                    cl[i * width : (i + 1) * width, col : col + LANES] = low
        part[device] = dot(ch[...], lag[0]) + dot(cl[...], lag[0]) + dot(ch[...], lag[1])

    piece = part.shape[1] // PIECES

    def hop(slot, k, landing, sem, target):
        at = pl.ds(k * piece, piece)
        return pltpu.make_async_remote_copy(
            src_ref=part.at[slot, at], dst_ref=landing.at[slot, at],
            send_sem=r_send.at[slot * PIECES + k], recv_sem=sem.at[slot * PIECES + k],
            device_id={"win": target}, device_id_type=MESH,
        )

    def finish(owner, half):
        slot = owner * 2 + half

        @pl.when(owner > row)
        def _():
            for k in range(PIECES):
                right = hop(slot, k, from_left, left_sem, row + 1)

                @pl.when(row > 0)
                def _():
                    right.wait_recv()
                    at = slice(k * piece, (k + 1) * piece)
                    part[slot, at] = part[slot, at] + from_left[slot, at]

                right.start()

        @pl.when(owner < row)
        def _():
            for k in range(PIECES):
                left = hop(slot, k, from_right, right_sem, row - 1)

                @pl.when(row < win_count - 1)
                def _():
                    left.wait_recv()
                    at = slice(k * piece, (k + 1) * piece)
                    part[slot, at] = part[slot, at] + from_right[slot, at]

                left.start()

    def step(q, _):
        owner, half, d = chunk_of(q)

        @pl.when(q == 2 * (1 - away))
        def _():
            gather[4].wait_recv()
            gather[6].start()
            gather[5].start()
            gather[2].wait_recv()
            gather[3].start()

        @pl.when(q == 2 * (2 - away))
        def _():
            gather[6].wait_recv()
            gather[7].start()

        @pl.when(lax.rem(q, 2) == 1)
        def _():
            pltpu.make_async_remote_copy(
                src_ref=gs.at[me], dst_ref=gs.at[me], send_sem=g_send.at[d], recv_sem=g_recv.at[d],
                device_id={"chan": lax.rem(me + 1, chan_count)}, device_id_type=MESH,
            ).wait_recv()

        compute(owner, half)

        @pl.when(inner == 0)
        def _():
            finish(owner, half)

        @pl.when((inner == 1) & (q >= 2) & (q < 4))
        def _():
            first, side, _ = chunk_of(q - 2)
            finish(first, side)

        return 0

    chunks = 2 * win_count
    lax.fori_loop(0, chunks, step, 0)

    back = 3 * upper

    def finish_back(when):
        @pl.when((inner == 1) & (when == 0))
        def _():
            for k in range(2):
                finish(back, core + k * (1 - 2 * core))

    parity = x + upper * (1 - 2 * x)
    finish_back(parity)

    @pl.when(inner == 1)
    def _():
        for q in (2, 3):
            owner, half, _ = chunk_of(q)
            finish(owner, half)

    finish_back(1 - parity)

    block = part.shape[1]
    for k in range(2):
        half = core + k * (1 - 2 * core)
        slot = row * 2 + half
        at = pl.ds(pl.multiple_of(half * block, block), block)
        out_ref[at, :] = part[slot]

        @pl.when(row < win_count - 1)
        def _():
            for j in range(PIECES):
                hop(slot, j, from_right, right_sem, row + 1).wait_recv()
            out_ref[at, :] += from_right[slot]

        @pl.when(row > 0)
        def _():
            for j in range(PIECES):
                hop(slot, j, from_left, left_sem, row - 1).wait_recv()
            out_ref[at, :] += from_left[slot]

    for copy in exchange + list(gather.values()):
        copy.wait_send()
    for slot in range(chunks):
        @pl.when(row != slot // 2)
        def _():
            for k in range(PIECES):
                hop(slot, k, from_left, left_sem, lax.rem(row + 1, win_count)).wait_send()


def fused(records, sources):
    chan_count, win_count = lax.axis_size("chan"), lax.axis_size("win")
    windows, time, channels = records.shape
    length = time * chan_count
    freq = length // 2
    width = channels // chan_count
    rows = windows * width
    source_count = sources.shape[0]
    lag_count = length // 4
    reach = length // 32
    half_width = min(16, time)
    owned = source_count // win_count
    factor = 1.0 / math.sqrt(windows * win_count * freq)
    fwd = forward_blocks(length, time)
    band = smooth_table(freq, reach)
    lag = lag_table(length, lag_count, factor)
    f32 = jnp.float32
    block = owned * width
    half = block // 2
    per_device = source_count // chan_count
    vmem = pl.BlockSpec(memory_space=pltpu.VMEM)
    hbm = pl.BlockSpec(memory_space=pltpu.HBM)
    out = pl.pallas_call(
        functools.partial(fused_kernel, half_width, reach, chan_count, win_count, per_device),
        out_shape=jax.ShapeDtypeStruct((block, lag_count), f32),
        in_specs=[pl.BlockSpec(memory_space=pltpu.SMEM), hbm, hbm, hbm, hbm],
        out_specs=vmem,
        scratch_shapes=[
            pltpu.VMEM(records.shape, f32),
            pltpu.VMEM((chan_count, rows, time), f32),
            pltpu.VMEM((chan_count, rows, time), f32),
            pltpu.VMEM((chan_count, rows, time), f32),
            pltpu.VMEM((4, rows, 2 * time), BF16),
            pltpu.VMEM((4, rows, 2 * time), BF16),
            pltpu.VMEM((rows, freq), BF16),
            pltpu.VMEM((rows, freq), BF16),
            pltpu.VMEM((rows, freq), f32),
            pltpu.VMEM((rows, freq), f32),
            pltpu.VMEM((chan_count, 2 * windows * per_device, freq), f32),
            pltpu.VMEM((half, 2 * freq), BF16),
            pltpu.VMEM((half, 2 * freq), BF16),
            pltpu.VMEM((2 * win_count, half, lag_count), f32),
            pltpu.VMEM((2 * win_count, half, lag_count), f32),
            pltpu.VMEM((2 * win_count, half, lag_count), f32),
            pltpu.VMEM(fwd.shape, BF16),
            pltpu.VMEM(band.shape, BF16),
            pltpu.VMEM(lag.shape, BF16),
            pltpu.SemaphoreType.DMA((windows,)),
            pltpu.SemaphoreType.DMA((3,)),
            pltpu.SemaphoreType.DMA((chan_count,)),
            pltpu.SemaphoreType.DMA((chan_count,)),
            pltpu.SemaphoreType.DMA((chan_count,)),
            pltpu.SemaphoreType.DMA((chan_count,)),
            pltpu.SemaphoreType.DMA((2 * win_count * PIECES,)),
            pltpu.SemaphoreType.DMA((2 * win_count * PIECES,)),
            pltpu.SemaphoreType.DMA((2 * win_count * PIECES,)),
        ],
        compiler_params=pltpu.CompilerParams(
            collective_id=0, has_side_effects=True, vmem_limit_bytes=66_400_000
        ),
        name="interferometry",
    )(sources, records, jnp.asarray(fwd), jnp.asarray(band), jnp.asarray(lag))
    return out.reshape(owned, width, lag_count).transpose(0, 2, 1)


def fits(records, sources):
    chan_count, win_count = lax.axis_size("chan"), lax.axis_size("win")
    time, channels = records.shape[1:]
    width = channels // chan_count
    return (
        time == LANES and chan_count == 8 and win_count == 4 and channels % LANES == 0
        and LANES % width == 0 and width % 16 == 0 and sources.shape[0] % chan_count == 0
    )


def body(records, sources):
    return fused(records, sources) if fits(records, sources) else local(records, sources)


def solution(mesh):
    placed = (P("win", "chan", None), P())
    return jax.shard_map(
        body, mesh=mesh, in_specs=placed, out_specs=P("win", None, "chan"), check_vma=False
    )
```
